256 devices in a mesh: vox: 64 (over z, x, core), chan: 4 (over y).
Axes of the slice: x: 4, y: 4, z: 8, core: 2. Of those that a mesh axis runs over, the one named last changes fastest.
Arguments:
- model_blocks: bfloat16 [23552, 128, 128], P(('vox', 'chan')), may hold values from -0.15625 to 0.15625
- start_image: float32 [2048, 32, 128], P('vox'), may hold values from 0 to 2
- measured: float32 [2048, 32, 128], P(('vox', 'chan')), may hold values from -6 to 6
- step_size: float32 [32], replicated, may hold values from 0.05 to 0.25
- sent_tiles: int32 [64, 64, 4], P('vox'), may hold values from -1 to 31, as said below
- block_rows: int32 [23552], P(('vox', 'chan')), may hold values from 0 to 7
- block_slots: int32 [23552], P(('vox', 'chan')), may hold values from 0 to 255, as said below
Outputs:
- estimate: float32 [2048, 32, 128], P('vox')
- residual: float32 [2048, 32, 128], P(('vox', 'chan'))
The draws below stay inside these ranges and needn't reach their ends.
Inputs may be any that keep to these rules, and one draw needn't show every extreme that they name: `sent_tiles`: an entry is -1 for an unused slot, else a tile of slab j; the used slots of one pair (j, v) come first, hold distinct tiles, number 1 to 4, and slab v always uses all 4 slots for itself. `block_slots`: every block names a used slot of its own device's vox index v, that is sent_tiles[j, v, s] is not -1.
All inputs are finite; a program needn't handle non-finite values.
Results may differ from the reference program's by a relative error of at most 0.0045.
Values may be sent and summed in bfloat16 or wider, within the bound.
A program may use at most 64 MiB of HBM per device.

```python
import math
import jax
import jax.numpy as jnp
from jax import lax

BLOCK_SIZE = 128
WAVELENGTHS = 32
TILES_DEV = 32
ROWS_DEV = 8
BLOCKS_DEV = 92
SLOT_CAP = 4
ITERATIONS = 4
ALL_TILES = 2048
ALL_ROWS = 2048
ALL_BLOCKS = 23552
N_VOX = 64
N_CHAN = 4


def slot_counts(key):
    inner_key = jax.random.fold_in(key, 7)
    first_key, second_key = jax.random.split(inner_key)
    height = jax.random.randint(first_key, (N_VOX, N_VOX), 0, SLOT_CAP)
    switch = jax.random.randint(second_key, (N_VOX, N_VOX), 0, 2)
    counts = 1 + height * switch
    diagonal = jnp.eye(N_VOX, dtype=jnp.int32)
    return (counts * (1 - diagonal) + SLOT_CAP * diagonal).astype(jnp.int32)


def draw_sent_tiles(key, part):
    counts = slot_counts(key)
    scores = jax.random.randint(jax.random.fold_in(key, 8), (N_VOX, N_VOX, TILES_DEV), 0, 1 << 20)
    scores = scores * TILES_DEV + jnp.arange(TILES_DEV, dtype=jnp.int32)
    ranking = jnp.argsort(scores, axis=-1, stable=True)[:, :, :SLOT_CAP].astype(jnp.int32)
    slot_range = jnp.arange(SLOT_CAP, dtype=jnp.int32)[None, None, :]
    return jnp.where(slot_range < counts[:, :, None], ranking, -1).astype(jnp.int32)


def draw_block_slots(key, part):
    counts = slot_counts(key)
    used_slots = (jnp.arange(SLOT_CAP, dtype=jnp.int32)[None, None, :] < counts[:, :, None]).astype(jnp.int32)
    by_target = jnp.transpose(used_slots, (1, 0, 2)).reshape(N_VOX, N_VOX * SLOT_CAP)
    running = jnp.cumsum(by_target, axis=1)
    totals = running[:, -1]
    per_vox = N_CHAN * BLOCKS_DEV
    limits = jnp.repeat(totals, per_vox).reshape(N_VOX, per_vox)
    picked_rank = jax.random.randint(jax.random.fold_in(key, 9), (N_VOX, per_vox), 0, limits)
    found = jax.vmap(lambda cumulative, wanted: jnp.searchsorted(cumulative, wanted, side='right'))(running, picked_rank)
    return found.reshape(N_VOX * per_vox).astype(jnp.int32)


def plant(entries, key, low, high):
    spot = [jax.random.randint(jax.random.fold_in(key, axis), (), 0, length) for axis, length in enumerate(entries.shape)]
    longest = entries.shape.index(max(entries.shape))
    neighbour = spot[:longest] + [(spot[longest] + 1) % entries.shape[longest]] + spot[longest + 1:]
    return entries.at[tuple(spot)].set(low).at[tuple(neighbour)].set(high)


def shard_levels(stream_key, extent, cuts, least, high):
    def one(position, shards_of):
        draws = jax.random.uniform(jax.random.fold_in(jax.random.fold_in(stream_key, 6), position), (shards_of,), jnp.float32, least / len(cuts), high / len(cuts))
        return jnp.repeat(jnp.exp(draws), extent[position] // shards_of).reshape((-1,) + (1,) * (len(extent) - position - 1))

    factor_of = one(*cuts[0])
    for cut in cuts[1:]:
        factor_of = factor_of * one(*cut)
    return factor_of


def noise(own_key, extent, spread, limit, shards=(), held_as=jnp.bfloat16):
    array = jax.random.normal(own_key, extent, jnp.float32) * spread
    if len(shards) > 0:
        array = shard_levels(own_key, extent, shards, -0.22, 0.18) * array
    return jnp.clip(array, min=-limit, max=limit).astype(held_as)


def setup_inputs(seed: int = 0) -> dict:
    splits = jax.random.split(jax.random.key(seed), 8)
    return {
        "model_blocks": noise(splits[0], (ALL_BLOCKS, BLOCK_SIZE, BLOCK_SIZE), (BLOCKS_DEV // ROWS_DEV * BLOCK_SIZE) ** -0.5, 0.15625, ((0, 256),)),
        "start_image": jnp.clip(2.0 * jax.random.uniform(splits[1], (ALL_TILES, WAVELENGTHS, BLOCK_SIZE), jnp.float32) ** shard_levels(splits[1], (ALL_TILES, WAVELENGTHS, BLOCK_SIZE), ((0, 64),), -0.2, 0.2), 0.0, 2.0),
        "measured": noise(splits[2], (ALL_ROWS, WAVELENGTHS, BLOCK_SIZE), 1.0, 6.0, ((0, 256),), jnp.float32),
        "step_size": jnp.clip(jnp.exp(jax.random.uniform(splits[3], (WAVELENGTHS,), jnp.float32, math.log(0.05), math.log(0.25))), 0.05, 0.25),
        "sent_tiles": draw_sent_tiles(jax.random.fold_in(splits[7], 71), 0),
        "block_rows": plant(jax.random.randint(splits[5], (ALL_BLOCKS,), 0, ROWS_DEV), jax.random.fold_in(splits[5], 1), 0, ROWS_DEV - 1).astype(jnp.int32),
        "block_slots": draw_block_slots(jax.random.fold_in(splits[7], 71), 0),
    }


def reference(model_blocks, start_image, measured, step_size, sent_tiles, block_rows, block_slots):
    devices = N_VOX * N_CHAN
    owner_dev = (jnp.arange(ALL_BLOCKS) // BLOCKS_DEV).astype(jnp.int32)
    holder_vox = (owner_dev // N_CHAN).astype(jnp.int32)
    source = (block_slots // SLOT_CAP).astype(jnp.int32)
    within = (block_slots % SLOT_CAP).astype(jnp.int32)
    tile_index = (source * TILES_DEV + sent_tiles[source, holder_vox, within]).astype(jnp.int32)
    blocks = model_blocks.reshape(devices, BLOCKS_DEV, BLOCK_SIZE, BLOCK_SIZE)
    tiles_by = tile_index.reshape(devices, BLOCKS_DEV)
    rows_by = block_rows.astype(jnp.int32).reshape(devices, BLOCKS_DEV)
    step_gains = step_size[None, :, None]
    estimate = start_image
    residual = measured
    for iteration in range(ITERATIONS):
        rounded = estimate.astype(jnp.bfloat16)

        def forward_one(inputs):
            blocks_here, tiles_here, rows_here = inputs
            picked = rounded[tiles_here].astype(jnp.float32)
            products = jnp.einsum("bwv,bsv->bws", picked, blocks_here.astype(jnp.float32), precision=lax.Precision.HIGHEST)
            return jax.ops.segment_sum(products, rows_here, num_segments=ROWS_DEV)

        predicted = lax.map(forward_one, (blocks, tiles_by, rows_by)).reshape(ALL_ROWS, WAVELENGTHS, BLOCK_SIZE)
        residual = measured - predicted
        narrow = residual.astype(jnp.bfloat16).reshape(devices, ROWS_DEV, WAVELENGTHS, BLOCK_SIZE)

        def adjoint_one(running_sum, inputs):
            blocks_here, tiles_here, rows_here, residual_here = inputs
            picked = residual_here[rows_here].astype(jnp.float32)
            adjoint_terms = jnp.einsum("bws,bsv->bwv", picked, blocks_here.astype(jnp.float32), precision=lax.Precision.HIGHEST)
            return running_sum.at[tiles_here].add(adjoint_terms), None

        gradient = lax.scan(adjoint_one, jnp.zeros(start_image.shape, jnp.float32), (blocks, tiles_by, rows_by, narrow))[0]
        estimate = jnp.maximum(estimate + step_gains * gradient, 0.0)
    return estimate, residual
```

```python
import functools

import jax
import jax.numpy as jnp
from jax import lax
from jax.experimental import pallas as pl
from jax.experimental.pallas import tpu as pltpu
from jax.sharding import PartitionSpec as P

ITERATIONS = 4
MESH = pl.DeviceIdType.MESH
VMEM = pl.BlockSpec(memory_space=pltpu.VMEM)
SMEM = pl.BlockSpec(memory_space=pltpu.SMEM)
ANY = pl.BlockSpec(memory_space=pl.ANY)


def exchange_body(vox, back, ahead, *refs):
    refs = list(refs)
    estimate_ref = refs.pop(0)
    if back:
        sums_ref, return_hot_ref, step_ref = refs.pop(0), refs.pop(0), refs.pop(0)
    if ahead:
        send_hot_ref = refs.pop(0)
    if back:
        new_estimate_ref = refs.pop(0)
    if ahead:
        arrived_ref = refs.pop(0)
    returned, outgoing, back_send, back_recv, out_send, out_recv = refs
    me = lax.axis_index("vox")
    barrier = pltpu.get_barrier_semaphore()

    def greet(step, carry):
        pl.semaphore_signal(
            barrier, inc=1, device_id={"vox": lax.rem(me + step, vox)}, device_id_type=MESH
        )
        return carry

    lax.fori_loop(1, vox, greet, 0)
    pl.semaphore_wait(barrier, vox - 1)

    def all_to_all(source, target, send_sem, recv_sem):
        def send(step, carry):
            peer = lax.rem(me + step, vox)
            pltpu.make_async_remote_copy(
                src_ref=source.at[peer],
                dst_ref=target.at[me],
                send_sem=send_sem,
                recv_sem=recv_sem,
                device_id={"vox": peer},
                device_id_type=MESH,
            ).start()
            return carry

        lax.fori_loop(1, vox, send, 0)
        target[me] = source[me]
        others = pl.ds(0, vox - 1)
        pltpu.make_async_copy(target.at[others], target.at[others], recv_sem).wait()
        pltpu.make_async_copy(source.at[others], source.at[others], send_sem).wait()

    estimate = estimate_ref[...]
    if back:
        all_to_all(sums_ref, returned, back_send, back_recv)
        gradient = jnp.dot(
            return_hot_ref[...],
            returned[...].reshape(-1, estimate.shape[-1]),
            preferred_element_type=jnp.float32,
        )
        estimate = jnp.maximum(estimate + step_ref[...] * gradient, 0.0)
        new_estimate_ref[...] = estimate
    if ahead:
        slots = jnp.dot(
            send_hot_ref[...], estimate.astype(jnp.bfloat16), preferred_element_type=jnp.float32
        )
        outgoing[...] = slots.astype(jnp.bfloat16).reshape(outgoing.shape)
        all_to_all(outgoing, arrived_ref, out_send, out_recv)


def exchange(vox, number, estimate, sums=None, return_hot=None, steps=None, send_hot=None):
    back, ahead = sums is not None, send_hot is not None
    width = estimate.shape[-1]
    packet = (vox, (return_hot if back else send_hot.T).shape[1] // vox, width)
    operands = [estimate]
    outs = []
    if back:
        operands += [sums, return_hot, steps]
        outs.append(jax.ShapeDtypeStruct(estimate.shape, jnp.float32))
    if ahead:
        operands.append(send_hot)
        outs.append(jax.ShapeDtypeStruct(packet, jnp.bfloat16))
    return pl.pallas_call(
        functools.partial(exchange_body, vox, back, ahead),
        out_shape=outs,
        in_specs=[VMEM] * len(operands),
        out_specs=[VMEM] * len(outs),
        scratch_shapes=[pltpu.VMEM(packet, jnp.bfloat16)] * 2 + [pltpu.SemaphoreType.DMA] * 4,
        compiler_params=pltpu.CompilerParams(
            collective_id=number, has_side_effects=True, vmem_limit_bytes=20 << 20
        ),
        name="exchange" + ("_back" if back else "") + ("_ahead" if ahead else ""),
    )(*operands)


def apply_body(sizes, unroll, *refs):
    count = len(sizes)
    slot_of, row_of, arrived_ref, measured_ref = refs[:4]
    models = refs[4 : 4 + count]
    sums_ref, residual_ref, tiles, held, predicted, narrow, sums, sems = refs[4 + count :]
    starts = [sum(sizes[:i]) for i in range(count)]
    copies = []
    for i, model in enumerate(models):
        copy = pltpu.make_async_copy(model, held.at[pl.ds(starts[i], sizes[i])], sems.at[i])
        copy.start()
        copies.append(copy)
    tiles[...] = arrived_ref[...].astype(jnp.float32).reshape(tiles.shape)
    sums[...] = jnp.zeros_like(sums)
    predicted[...] = jnp.zeros_like(predicted)
    for copy in copies:
        copy.wait()
    total = sum(sizes)

    def forward(step, carry):
        for u in range(unroll):
            k = (step * unroll + u) * 2
            left = jnp.concatenate([tiles[slot_of[k]], tiles[slot_of[k + 1]]], axis=0)
            right = held[pl.ds(k, 2)].reshape(2 * held.shape[1], held.shape[2])
            product = lax.dot_general(
                left.astype(jnp.bfloat16),
                right,
                (((1,), (1,)), ((), ())),
                preferred_element_type=jnp.float32,
            )
            half, width = tiles.shape[1], held.shape[1]
            predicted[row_of[k]] += product[:half, :width]
            predicted[row_of[k + 1]] += product[half:, width:]
        return carry

    lax.fori_loop(0, total // 2 // unroll, forward, 0)
    residual = measured_ref[...] - predicted[...]
    residual_ref[...] = residual
    narrow[...] = residual.astype(jnp.bfloat16).astype(jnp.float32)

    def adjoint(step, carry):
        for u in range(unroll):
            k = (step * unroll + u) * 2
            left = jnp.concatenate([narrow[row_of[k]], narrow[row_of[k + 1]]], axis=0)
            right = jnp.concatenate([held[k], held[k + 1]], axis=1)
            product = jnp.dot(left.astype(jnp.bfloat16), right, preferred_element_type=jnp.float32)
            half, width = tiles.shape[1], held.shape[2]
            sums[slot_of[k]] += product[:half, :width]
            sums[slot_of[k + 1]] += product[half:, width:]
        return carry

    lax.fori_loop(0, total // 2 // unroll, adjoint, 0)
    sums_ref[...] = sums[...].reshape(sums_ref.shape).astype(jnp.bfloat16)


def apply(slot_of, row_of, arrived, measured, models):
    sizes = [model.shape[0] for model in models]
    total = sum(sizes)
    block = models[0].shape[1:]
    waves, width = measured.shape[1:]
    slots = arrived.size // (waves * width)
    unroll = max(u for u in range(1, 24) if (total // 2) % u == 0)
    return pl.pallas_call(
        functools.partial(apply_body, sizes, unroll),
        out_shape=(
            jax.ShapeDtypeStruct(arrived.shape, jnp.bfloat16),
            jax.ShapeDtypeStruct(measured.shape, jnp.float32),
        ),
        in_specs=[SMEM, SMEM, VMEM, VMEM] + [ANY] * len(models),
        out_specs=(VMEM, VMEM),
        scratch_shapes=[
            pltpu.VMEM((slots, waves, width), jnp.float32),
            pltpu.VMEM((total,) + block, jnp.bfloat16),
            pltpu.VMEM(measured.shape, jnp.float32),
            pltpu.VMEM(measured.shape, jnp.float32),
            pltpu.VMEM((slots, waves, width), jnp.float32),
            pltpu.SemaphoreType.DMA((len(models),)),
        ],
        compiler_params=pltpu.CompilerParams(vmem_limit_bytes=40 << 20),
        name="apply_blocks",
    )(slot_of, row_of, arrived, measured, *models)


def shards(model_blocks, start_image, measured, step_size, sent_tiles, block_rows, block_slots):
    vox, chan = lax.axis_size("vox"), lax.axis_size("chan")
    channel = lax.axis_index("chan")
    send_table = sent_tiles[0]
    capacity = send_table.shape[1]
    tile_count, wave_count, width = start_image.shape
    row_count = measured.shape[0]
    waves = wave_count // chan

    def shift(value, by):
        return lax.ppermute(value, "chan", [(c, (c + by) % chan) for c in range(chan)])

    block_count = model_blocks.shape[0]
    half = block_count // 2
    from_left = shift(model_blocks, 1)
    from_right = shift(model_blocks, -1)
    far_low = shift(from_left[:half], 1)
    far_high = shift(from_right[half:], -1)
    models = [model_blocks, from_left, from_right, far_low, far_high]
    code = block_slots * row_count + block_rows
    codes = [code, shift(code, 1), shift(code, -1), shift(code, 2)]
    slot_of = jnp.concatenate([c // row_count for c in codes])
    row_of = jnp.concatenate([i * row_count + c % row_count for i, c in enumerate(codes)])
    quarters = measured.reshape(row_count, chan, waves, width)

    def quarter(by):
        return lax.dynamic_index_in_dim(quarters, (channel + by) % chan, axis=1, keepdims=False)

    group_measured = jnp.concatenate(
        [quarter(0), shift(quarter(1), 1), shift(quarter(-1), -1), shift(quarter(2), 2)]
    )

    estimate = lax.dynamic_slice_in_dim(start_image, channel * waves, waves, axis=1)
    estimate = estimate.reshape(tile_count * waves, width)
    steps = lax.dynamic_slice_in_dim(step_size, channel * waves, waves)
    steps = jnp.broadcast_to(jnp.tile(steps, tile_count)[:, None], estimate.shape)
    tile_of = jnp.repeat(jnp.arange(tile_count, dtype=jnp.int32), waves)
    wave_of = jnp.tile(jnp.arange(waves, dtype=jnp.int32), tile_count)
    slot_tile = jnp.repeat(send_table.reshape(-1), waves)
    slot_wave = jnp.tile(jnp.arange(waves, dtype=jnp.int32), vox * capacity)
    return_hot = (
        (tile_of[:, None] == slot_tile[None, :]) & (wave_of[:, None] == slot_wave[None, :])
    ).astype(jnp.bfloat16)
    send_hot = (
        (slot_tile[:, None] == tile_of[None, :]) & (slot_wave[:, None] == wave_of[None, :])
    ).astype(jnp.bfloat16)

    (arrived,) = exchange(vox, 0, estimate, send_hot=send_hot)
    for iteration in range(ITERATIONS):
        sums, residual = apply(slot_of, row_of, arrived, group_measured, models)
        if iteration < ITERATIONS - 1:
            estimate, arrived = exchange(vox, 1, estimate, sums, return_hot, steps, send_hot)
        else:
            (estimate,) = exchange(vox, 2, estimate, sums, return_hot, steps)

    parts = residual.reshape(chan, row_count, waves, width)
    own_rows = [parts[0], shift(parts[1], -1), shift(parts[3], 2), shift(parts[2], 1)]
    estimate = estimate.reshape(tile_count, waves, width)
    whole = [estimate] + [shift(estimate, -by) for by in range(1, chan)]

    def join(pieces):
        ordered = jnp.roll(jnp.stack(pieces, axis=1), channel, axis=1)
        return ordered.reshape(pieces[0].shape[0], chan * waves, width)

    return (join(whole), join(own_rows))


def solution(mesh):
    in_specs = (
        P(("vox", "chan"), None, None),
        P("vox", None, None),
        P(("vox", "chan"), None, None),
        P(),
        P("vox", None, None),
        P(("vox", "chan")),
        P(("vox", "chan")),
    )
    out_specs = (P("vox", None, None), P(("vox", "chan"), None, None))
    return jax.shard_map(shards, mesh=mesh, in_specs=in_specs, out_specs=out_specs, check_vma=False)
```

```python
import functools

import jax
import jax.numpy as jnp
from jax import lax
from jax.experimental import pallas as pl
from jax.experimental.pallas import tpu as pltpu
from jax.sharding import PartitionSpec as P

ITERATIONS = 4
STREAMS = 2
MESH = pl.DeviceIdType.MESH
VMEM = pl.BlockSpec(memory_space=pltpu.VMEM)
ANY = pl.BlockSpec(memory_space=pl.ANY)


def landweber_body(
    vox,
    chan,
    model_ref,
    gather_ref,
    scatter_ref,
    start_ref,
    measured_ref,
    steps_ref,
    send_hot_ref,
    return_hot_ref,
    row_hot_ref,
    row_sum_ref,
    estimate_out,
    residual_out,
    held,
    gather_hot,
    scatter_hot,
    estimate,
    outgoing,
    arrived,
    picked,
    tiles,
    high,
    low,
    narrow,
    terms,
    group_terms,
    slot_sums,
    returned,
    load_sems,
    ahead_send,
    ahead_recv,
    tile_send,
    tile_recv,
    term_send,
    term_recv,
    back_send,
    back_recv,
    final_send,
    final_recv,
):
    me, channel = lax.axis_index("vox"), lax.axis_index("chan")
    peers = range(1, chan)
    block_count, samples, voxels = held.shape
    rows = tiles.shape[2]
    waves = rows // block_count
    pack = 16 // waves
    f32, bf16 = jnp.float32, jnp.bfloat16

    def vox_peer(step):
        return lax.rem(me + step, vox)

    def chan_peer(step):
        return lax.rem(channel + step, chan)

    barrier = pltpu.get_barrier_semaphore()

    def greet(step, carry):
        pl.semaphore_signal(barrier, inc=1, device_id={"vox": vox_peer(step)}, device_id_type=MESH)
        return carry

    lax.fori_loop(1, vox, greet, 0)
    for p in peers:
        pl.semaphore_signal(barrier, inc=1, device_id={"chan": chan_peer(p)}, device_id_type=MESH)

    loads = [
        pltpu.make_async_copy(source, target, load_sems.at[i])
        for i, (source, target) in enumerate(
            [(gather_ref, gather_hot), (model_ref, held), (scatter_ref, scatter_hot)]
        )
    ]
    for load in loads:
        load.start()

    estimate[...] = start_ref[...]
    high[rows * chan :, :] = jnp.zeros_like(high[rows * chan :, :])
    low[rows * chan :, :] = jnp.zeros_like(low[rows * chan :, :])
    for p in range(chan):
        tail = group_terms.shape[2] - rows
        group_terms[:, p, rows:, :] = jnp.zeros((STREAMS, tail, voxels), bf16)

    def start_vox(source, target, send_sem, recv_sem, g):
        def send(step, carry):
            peer = vox_peer(step)
            pltpu.make_async_remote_copy(
                src_ref=source.at[g, peer],
                dst_ref=target.at[g, me],
                send_sem=send_sem.at[g],
                recv_sem=recv_sem.at[g],
                device_id={"vox": peer},
                device_id_type=MESH,
            ).start()
            return carry

        lax.fori_loop(1, vox, send, 0)
        target[g, me] = source[g, me]

    def wait_vox(source, target, send_sem, recv_sem, g):
        others = pl.ds(0, vox - 1)
        pltpu.make_async_copy(target.at[g, others], target.at[g, others], recv_sem.at[g]).wait()
        pltpu.make_async_copy(source.at[g, others], source.at[g, others], send_sem.at[g]).wait()

    def chan_copy(source, target, send_sem, recv_sem, g, p):
        return pltpu.make_async_remote_copy(
            src_ref=source.at[g, p],
            dst_ref=target.at[g, chan - p, pl.ds(0, rows)],
            send_sem=send_sem.at[g, p],
            recv_sem=recv_sem.at[g, chan - p],
            device_id={"chan": chan_peer(p)},
            device_id_type=MESH,
        )

    def wait_chan(source, target, send_sem, recv_sem, g):
        for p in peers:
            landed = target.at[g, p, pl.ds(0, rows)]
            pltpu.make_async_copy(landed, landed, recv_sem.at[g, p]).wait()
            pltpu.make_async_copy(source.at[g, p], source.at[g, p], send_sem.at[g, p]).wait()

    def start_ahead(g):
        slots = jnp.dot(
            send_hot_ref[...], estimate[g].astype(bf16), preferred_element_type=f32
        )
        outgoing[g] = slots.astype(bf16).reshape(outgoing.shape[1:])

    def send_ahead(g):
        start_vox(outgoing, arrived, ahead_send, ahead_recv, g)

    for g in range(STREAMS):
        start_ahead(g)
    pl.semaphore_wait(barrier, vox - 1 + chan - 1)
    for g in range(STREAMS):
        send_ahead(g)
    loads[0].wait()

    upper = lax.broadcasted_iota(jnp.int32, (8, voxels), 0) < waves

    def diagonal(product, p):
        base = 16 * p
        halves = []
        for h in range(2):
            part = slice(base + 8 * h, base + 8 * h + 8)
            first = product[part, (2 * h) * voxels : (2 * h + 1) * voxels]
            second = product[part, (2 * h + 1) * voxels : (2 * h + 2) * voxels]
            halves.append(jnp.where(upper, first, second))
        return jnp.concatenate(halves, axis=0)

    def pick_tiles(g, carry):
        wait_vox(outgoing, arrived, ahead_send, ahead_recv, g)
        source = arrived[g].reshape(-1, voxels)
        for p in list(peers) + [0]:
            part = jnp.dot(
                gather_hot[p * rows : (p + 1) * rows, :], source, preferred_element_type=f32
            ).astype(bf16)
            if p == 0:
                tiles[g, 0] = part
            else:
                picked[g, p] = part
                chan_copy(picked, tiles, tile_send, tile_recv, g, p).start()
        return carry

    def apply(g, carry):
        wait_chan(picked, tiles, tile_send, tile_recv, g)
        for q in range(block_count // pack):
            span = slice(16 * q, 16 * q + 16)
            left = jnp.concatenate([tiles[g, p, span, :] for p in range(chan)], axis=0)
            right = held[pack * q : pack * (q + 1)].reshape(pack * samples, voxels)
            product = lax.dot_general(
                left, right, (((1,), (1,)), ((), ())), preferred_element_type=f32
            )
            for p in range(chan):
                piece = diagonal(product, p)
                top = piece.astype(bf16)
                where = slice(p * rows + 16 * q, p * rows + 16 * q + 16)
                high[where, :] = top
                low[where, :] = (piece - top.astype(f32)).astype(bf16)
        predicted = jnp.dot(row_sum_ref[...], high[...], preferred_element_type=f32)
        predicted += jnp.dot(row_sum_ref[...], low[...], preferred_element_type=f32)
        part = predicted.shape[0] // chan
        residuals = []
        for p in range(chan):
            residual = measured_ref[chan_peer(p), g] - predicted[p * part : (p + 1) * part]
            residual_out[chan_peer(p), g] = residual
            residuals.append(residual.astype(bf16))
        narrow[...] = jnp.dot(
            row_hot_ref[...], jnp.concatenate(residuals, axis=0), preferred_element_type=f32
        ).astype(bf16)
        for q in range(block_count // pack):
            left = jnp.concatenate(
                [narrow[p * rows + 16 * q : p * rows + 16 * q + 16, :] for p in range(chan)], axis=0
            )
            right = jnp.concatenate([held[pack * q + i] for i in range(pack)], axis=1)
            product = jnp.dot(left, right, preferred_element_type=f32)
            for p in range(chan):
                piece = diagonal(product, p).astype(bf16)
                if p == 0:
                    group_terms[g, 0, 16 * q : 16 * q + 16, :] = piece
                else:
                    terms[g, p, 16 * q : 16 * q + 16, :] = piece
        for p in peers:
            chan_copy(terms, group_terms, term_send, term_recv, g, p).start()
        return carry

    def sum_slots(g, carry):
        wait_chan(terms, group_terms, term_send, term_recv, g)
        source = group_terms[g].reshape(-1, voxels)
        chunk = 256
        packets = chunk // slot_sums.shape[2]
        for i in range(scatter_hot.shape[0] // chunk):
            part = jnp.dot(
                scatter_hot[i * chunk : (i + 1) * chunk, :], source, preferred_element_type=f32
            )
            slot_sums[g, i * packets : (i + 1) * packets] = part.astype(bf16).reshape(
                (packets,) + slot_sums.shape[2:]
            )
        start_vox(slot_sums, returned, back_send, back_recv, g)
        return carry

    def update(g):
        wait_vox(slot_sums, returned, back_send, back_recv, g)
        gradient = jnp.dot(
            return_hot_ref[...], returned[g].reshape(-1, voxels), preferred_element_type=f32
        )
        estimate[g] = jnp.maximum(estimate[g] + steps_ref[g] * gradient, 0.0)

    def update_and_send(g, carry):
        update(g)
        start_ahead(g)
        send_ahead(g)
        return carry

    def iterate(iteration, carry):
        lax.fori_loop(0, STREAMS, pick_tiles, 0)

        @pl.when(iteration == 0)
        def _():
            for load in loads[1:]:
                load.wait()

        lax.fori_loop(0, STREAMS, apply, 0)
        lax.fori_loop(0, STREAMS, sum_slots, 0)

        @pl.when(iteration < ITERATIONS - 1)
        def _():
            lax.fori_loop(0, STREAMS, update_and_send, 0)

        return carry

    lax.fori_loop(0, ITERATIONS, iterate, 0)

    def final_copy(g, p):
        return pltpu.make_async_remote_copy(
            src_ref=estimate.at[g],
            dst_ref=estimate_out.at[channel, g],
            send_sem=final_send.at[g, p],
            recv_sem=final_recv.at[g, chan - p],
            device_id={"chan": chan_peer(p)},
            device_id_type=MESH,
        )

    for g in range(STREAMS):
        update(g)
        for p in peers:
            final_copy(g, p).start()
        estimate_out[channel, g] = estimate[g]
    for g in range(STREAMS):
        for p in peers:
            landed = estimate_out.at[chan_peer(p), g]
            pltpu.make_async_copy(landed, landed, final_recv.at[g, p]).wait()
            pltpu.make_async_copy(estimate.at[g], estimate.at[g], final_send.at[g, p]).wait()


def shards(model_blocks, start_image, measured, step_size, sent_tiles, block_rows, block_slots):
    vox, chan = lax.axis_size("vox"), lax.axis_size("chan")
    channel = lax.axis_index("chan")
    send_table = sent_tiles[0]
    capacity = send_table.shape[1]
    tile_count, wave_count, width = start_image.shape
    row_count, block_count = measured.shape[0], model_blocks.shape[0]
    waves = wave_count // chan // STREAMS
    slots = vox * capacity
    rows = block_count * waves
    padded = -(-rows // 128) * 128
    int32, bf16 = jnp.int32, jnp.bfloat16

    def shift(value, by):
        return lax.ppermute(value, "chan", [(c, (c + by) % chan) for c in range(chan)])

    def flat(index, minor):
        spread = index[..., None] * minor + jnp.arange(minor, dtype=int32)
        return jnp.where(index[..., None] < 0, -1, spread).reshape(index.shape[:-1] + (-1,))

    peer_slots = jnp.stack([block_slots] + [shift(block_slots, -p) for p in range(1, chan)])
    slot_code = flat(peer_slots, waves)
    gather_hot = (slot_code.reshape(-1)[:, None] == jnp.arange(slots * waves)[None, :]).astype(bf16)
    slot_code = jnp.pad(slot_code, ((0, 0), (0, padded - rows)), constant_values=-1)
    scatter_hot = (
        jnp.arange(slots * waves)[:, None] == slot_code.reshape(-1)[None, :]
    ).astype(bf16)
    send_code = flat(send_table.reshape(-1), waves)
    tile_range = jnp.arange(tile_count * waves)
    send_hot = (send_code[:, None] == tile_range[None, :]).astype(bf16)
    return_hot = (tile_range[:, None] == send_code[None, :]).astype(bf16)
    row_code = flat(
        jnp.arange(chan, dtype=int32)[:, None] * row_count + block_rows[None, :], waves
    ).reshape(-1)
    row_range = jnp.arange(chan * row_count * waves)
    row_hot = (row_code[:, None] == row_range[None, :]).astype(bf16)
    row_code = jnp.pad(row_code, (0, chan * (padded - rows)), constant_values=-1)
    row_sum = (row_range[:, None] == row_code[None, :]).astype(bf16)

    own = lax.dynamic_slice_in_dim(start_image, channel * waves * STREAMS, waves * STREAMS, axis=1)
    own = own.reshape(tile_count, STREAMS, waves, width).transpose(1, 0, 2, 3)
    own = own.reshape(STREAMS, tile_count * waves, width)
    steps = lax.dynamic_slice_in_dim(step_size, channel * waves * STREAMS, waves * STREAMS)
    steps = jnp.tile(steps.reshape(STREAMS, waves), (1, tile_count))
    steps = jnp.broadcast_to(steps[:, :, None], own.shape)
    split = measured.reshape(row_count, chan, STREAMS, waves, width).transpose(1, 2, 0, 3, 4)
    split = split.reshape(chan, STREAMS, row_count * waves, width)

    packet = (STREAMS, vox, capacity * waves, width)
    quarter = (STREAMS, chan, rows, width)
    dma = pltpu.SemaphoreType.DMA
    estimate, residual = pl.pallas_call(
        functools.partial(landweber_body, vox, chan),
        out_shape=(
            jax.ShapeDtypeStruct((chan,) + own.shape, jnp.float32),
            jax.ShapeDtypeStruct(split.shape, jnp.float32),
        ),
        in_specs=[ANY] * 3 + [VMEM] * 7,
        out_specs=(VMEM, VMEM),
        scratch_shapes=[
            pltpu.VMEM(model_blocks.shape, bf16),
            pltpu.VMEM(gather_hot.shape, bf16),
            pltpu.VMEM(scatter_hot.shape, bf16),
            pltpu.VMEM(own.shape, jnp.float32),
            pltpu.VMEM(packet, bf16),
            pltpu.VMEM(packet, bf16),
            pltpu.VMEM(quarter, bf16),
            pltpu.VMEM(quarter, bf16),
            pltpu.VMEM((chan * padded, width), bf16),
            pltpu.VMEM((chan * padded, width), bf16),
            pltpu.VMEM((chan * rows, width), bf16),
            pltpu.VMEM(quarter, bf16),
            pltpu.VMEM((STREAMS, chan, padded, width), bf16),
            pltpu.VMEM(packet, bf16),
            pltpu.VMEM(packet, bf16),
            dma((3,)),
            dma((STREAMS,)),
            dma((STREAMS,)),
            dma((STREAMS, chan)),
            dma((STREAMS, chan)),
            dma((STREAMS, chan)),
            dma((STREAMS, chan)),
            dma((STREAMS,)),
            dma((STREAMS,)),
            dma((STREAMS, chan)),
            dma((STREAMS, chan)),
        ],
        compiler_params=pltpu.CompilerParams(
            collective_id=0, has_side_effects=True, vmem_limit_bytes=32 << 20
        ),
        name="landweber",
    )(
        model_blocks,
        gather_hot,
        scatter_hot,
        own,
        split,
        steps,
        send_hot,
        return_hot,
        row_hot,
        row_sum,
    )
    estimate = estimate.reshape(chan, STREAMS, tile_count, waves, width).transpose(2, 0, 1, 3, 4)
    residual = residual.reshape(chan, STREAMS, row_count, waves, width).transpose(2, 0, 1, 3, 4)
    return (
        estimate.reshape(tile_count, wave_count, width),
        residual.reshape(row_count, wave_count, width),
    )


def solution(mesh):
    in_specs = (
        P(("vox", "chan"), None, None),
        P("vox", None, None),
        P(("vox", "chan"), None, None),
        P(),
        P("vox", None, None),
        P(("vox", "chan")),
        P(("vox", "chan")),
    )
    out_specs = (P("vox", None, None), P(("vox", "chan"), None, None))
    return jax.shard_map(shards, mesh=mesh, in_specs=in_specs, out_specs=out_specs, check_vma=False)
```

```python
import functools

import jax
import jax.numpy as jnp
from jax import lax
from jax.experimental import pallas as pl
from jax.experimental.pallas import tpu as pltpu
from jax.sharding import PartitionSpec as P

ITERATIONS = 4
STREAMS = 2
PLANE = 8
LANES = 128
MESH = pl.DeviceIdType.MESH
VMEM = pl.BlockSpec(memory_space=pltpu.VMEM)
ANY = pl.BlockSpec(memory_space=pl.ANY)


def landweber_body(
    vox,
    chan,
    model_ref,
    slots_ref,
    start_ref,
    measured_ref,
    steps_ref,
    send_hot_ref,
    return_hot_ref,
    row_hot_ref,
    row_sum_ref,
    estimate_out,
    residual_out,
    held,
    peer_slots,
    gather_hot,
    scatter_hot,
    estimate,
    outgoing,
    arrived,
    spread,
    picked,
    tiles,
    high,
    low,
    narrow,
    terms,
    group_terms,
    stacked,
    slot_sums,
    returned,
    load_sem,
    slots_send,
    slots_recv,
    ahead_send,
    ahead_recv,
    tile_send,
    tile_recv,
    term_send,
    term_recv,
    back_send,
    back_recv,
    final_send,
    final_recv,
):
    me, channel = lax.axis_index("vox"), lax.axis_index("chan")
    layer, place = me // PLANE, lax.rem(me, PLANE)
    layers = vox // PLANE
    peers = (2, 1, 3)
    padded, samples, voxels = held.shape
    block_count = model_ref.shape[0]
    rows = tiles.shape[2]
    waves = rows // padded
    pack = 8 // waves
    slot_count = scatter_hot.shape[0]
    f32, bf16 = jnp.float32, jnp.bfloat16

    def chan_peer(step):
        return lax.rem(channel + step, chan)

    barrier = pltpu.get_barrier_semaphore()

    def greet(step, carry):
        peer = lax.rem(me + step, vox)
        pl.semaphore_signal(barrier, inc=1, device_id={"vox": peer}, device_id_type=MESH)
        return carry

    lax.fori_loop(1, vox, greet, 0)
    for p in peers:
        pl.semaphore_signal(barrier, inc=1, device_id={"chan": chan_peer(p)}, device_id_type=MESH)

    load = pltpu.make_async_copy(model_ref, held.at[pl.ds(0, block_count)], load_sem)
    load.start()

    def start_vox(source, target, send_sem, recv_sem, g):
        def send(distance):
            def one(turn, carry):
                for d in distance:
                    peer = lax.rem(layer + d, layers) * PLANE + lax.rem(place + turn, PLANE)
                    pltpu.make_async_remote_copy(
                        src_ref=source.at[g, peer],
                        dst_ref=target.at[g, me],
                        send_sem=send_sem.at[g],
                        recv_sem=recv_sem.at[g],
                        device_id={"vox": peer},
                        device_id_type=MESH,
                    ).start()
                return carry

            return one

        half = layers // 2
        lax.fori_loop(0, PLANE, send((half,)), 0)
        for d in range(half - 1, 0, -1):
            lax.fori_loop(0, PLANE, send((d, layers - d)), 0)
        lax.fori_loop(1, PLANE, send((0,)), 0)
        target[g, me] = source[g, me]

    def wait_vox(source, target, send_sem, recv_sem, g):
        others = pl.ds(0, vox - 1)
        pltpu.make_async_copy(target.at[g, others], target.at[g, others], recv_sem.at[g]).wait()
        pltpu.make_async_copy(source.at[g, others], source.at[g, others], send_sem.at[g]).wait()

    def chan_copy(source, target, send_sem, recv_sem, g, p):
        return pltpu.make_async_remote_copy(
            src_ref=source.at[g, p],
            dst_ref=target.at[g, chan - p],
            send_sem=send_sem.at[g, p],
            recv_sem=recv_sem.at[g, chan - p],
            device_id={"chan": chan_peer(p)},
            device_id_type=MESH,
        )

    def wait_chan(source, target, send_sem, recv_sem, g):
        for p in peers:
            pltpu.make_async_copy(target.at[g, p], target.at[g, p], recv_sem.at[g, p]).wait()
            pltpu.make_async_copy(source.at[g, p], source.at[g, p], send_sem.at[g, p]).wait()

    def start_ahead(g):
        slots = jnp.dot(
            send_hot_ref[...], estimate[g].astype(bf16), preferred_element_type=f32
        )
        outgoing[g] = slots.reshape(outgoing.shape[1:]).astype(bf16)

    def send_ahead(g):
        start_vox(outgoing, arrived, ahead_send, ahead_recv, g)

    def slots_copy(p):
        return pltpu.make_async_remote_copy(
            src_ref=slots_ref,
            dst_ref=peer_slots.at[chan - p],
            send_sem=slots_send.at[p],
            recv_sem=slots_recv.at[chan - p],
            device_id={"chan": chan_peer(p)},
            device_id_type=MESH,
        )

    estimate[...] = start_ref[...]
    for g in range(STREAMS):
        start_ahead(g)
    pl.semaphore_wait(barrier, vox - 1 + chan - 1)
    for p in peers:
        slots_copy(p).start()

    def first_send(g, carry):
        send_ahead(g)
        return carry

    lax.fori_loop(0, STREAMS, first_send, 0)
    held[block_count:] = jnp.zeros((padded - block_count, samples, voxels), bf16)
    stacked[...] = jnp.zeros_like(stacked)
    peer_slots[0] = slots_ref[...]
    for p in peers:
        pltpu.make_async_copy(peer_slots.at[p], peer_slots.at[p], slots_recv.at[p]).wait()
        pltpu.make_async_copy(slots_ref, slots_ref, slots_send.at[p]).wait()
    slot_range = lax.broadcasted_iota(jnp.int32, (slot_count, LANES), 0)
    diagonal_hot = jnp.where(
        lax.broadcasted_iota(jnp.int32, (LANES, LANES), 0)
        == lax.broadcasted_iota(jnp.int32, (LANES, LANES), 1),
        1.0,
        0.0,
    ).astype(bf16)
    for p in range(chan):
        span = slice(p * LANES, (p + 1) * LANES)
        named = jnp.broadcast_to(peer_slots[p][0:1, :], slot_range.shape)
        hot = jnp.where(slot_range == named, 1.0, 0.0).astype(bf16)
        scatter_hot[:, span] = hot
        gather_hot[span, :] = lax.dot_general(
            diagonal_hot, hot, (((1,), (1,)), ((), ())), preferred_element_type=f32
        ).astype(bf16)
    load.wait()

    group_of = lax.broadcasted_iota(jnp.int32, (8, voxels), 0) // waves

    def diagonal(product, p):
        part = slice(8 * p, 8 * p + 8)
        piece = product[part, 0:voxels]
        for i in range(1, pack):
            piece = jnp.where(group_of == i, product[part, i * voxels : (i + 1) * voxels], piece)
        return piece

    def pick_tiles(g):
        wait_vox(outgoing, arrived, ahead_send, ahead_recv, g)
        spread[0 : slot_count * waves, :] = arrived[g].astype(f32).reshape(-1, voxels)
        source = jnp.concatenate(
            [spread[pl.ds(w, slot_count, stride=waves), :] for w in range(waves)], axis=1
        ).astype(bf16)
        product = jnp.dot(gather_hot[...], source, preferred_element_type=f32)
        for p in peers + (0,):
            for w in range(waves):
                spread[pl.ds(p * rows + w, padded, stride=waves), :] = product[
                    p * LANES : p * LANES + padded, w * voxels : (w + 1) * voxels
                ]
            part = spread[p * rows : (p + 1) * rows, :].astype(bf16)
            if p == 0:
                tiles[g, 0] = part
            else:
                picked[g, p] = part
                chan_copy(picked, tiles, tile_send, tile_recv, g, p).start()

    def apply(g):
        wait_chan(picked, tiles, tile_send, tile_recv, g)
        for q in range(rows // 16):
            wide = [tiles[g, p, 16 * q : 16 * q + 16, :].astype(f32) for p in range(chan)]
            halves = []
            for h in range(2):
                left = jnp.concatenate([w[8 * h : 8 * h + 8] for w in wide], axis=0).astype(bf16)
                k = (2 * q + h) * pack
                right = held[k : k + pack].reshape(pack * samples, voxels)
                product = lax.dot_general(
                    left, right, (((1,), (1,)), ((), ())), preferred_element_type=f32
                )
                halves.append([diagonal(product, p) for p in range(chan)])
            for p in range(chan):
                piece = jnp.concatenate([halves[0][p], halves[1][p]], axis=0)
                top = piece.astype(bf16)
                where = slice(p * rows + 16 * q, p * rows + 16 * q + 16)
                high[where, :] = top
                low[where, :] = (piece - top.astype(f32)).astype(bf16)
        predicted = jnp.dot(row_sum_ref[...], high[...], preferred_element_type=f32)
        predicted += jnp.dot(row_sum_ref[...], low[...], preferred_element_type=f32)
        part = predicted.shape[0] // chan
        residuals = []
        for p in range(chan):
            residual = measured_ref[chan_peer(p), g] - predicted[p * part : (p + 1) * part]
            residual_out[chan_peer(p), g] = residual
            residuals.append(residual.astype(bf16))
        if LANES > chan * part:
            residuals.append(jnp.zeros((LANES - chan * part, samples), bf16))
        narrow[...] = jnp.dot(
            row_hot_ref[...], jnp.concatenate(residuals, axis=0), preferred_element_type=f32
        )
        for q in range(rows // 16):
            halves = []
            for h in range(2):
                k = (2 * q + h) * pack
                left = jnp.concatenate(
                    [
                        narrow[p * rows + 16 * q + 8 * h : p * rows + 16 * q + 8 * h + 8, :]
                        for p in range(chan)
                    ],
                    axis=0,
                ).astype(bf16)
                right = jnp.concatenate([held[k + i] for i in range(pack)], axis=1)
                product = jnp.dot(left, right, preferred_element_type=f32)
                halves.append([diagonal(product, p) for p in range(chan)])
            for p in range(chan):
                piece = jnp.concatenate([halves[0][p], halves[1][p]], axis=0).astype(bf16)
                if p == 0:
                    group_terms[g, 0, 16 * q : 16 * q + 16, :] = piece
                else:
                    terms[g, p, 16 * q : 16 * q + 16, :] = piece
        for p in peers:
            chan_copy(terms, group_terms, term_send, term_recv, g, p).start()

    def sum_slots(g):
        wait_chan(terms, group_terms, term_send, term_recv, g)
        for p in range(chan):
            spread[p * rows : (p + 1) * rows, :] = group_terms[g, p].astype(f32)
            for w in range(waves):
                stacked[p * LANES : p * LANES + padded, w * voxels : (w + 1) * voxels] = spread[
                    pl.ds(p * rows + w, padded, stride=waves), :
                ].astype(bf16)
        product = jnp.dot(scatter_hot[...], stacked[...], preferred_element_type=f32)
        for w in range(waves):
            spread[pl.ds(w, slot_count, stride=waves), :] = product[:, w * voxels : (w + 1) * voxels]
        slot_sums[g] = (
            spread[0 : slot_count * waves, :].reshape(slot_sums.shape[1:]).astype(bf16)
        )
        start_vox(slot_sums, returned, back_send, back_recv, g)

    def final_copy(g, p):
        return pltpu.make_async_remote_copy(
            src_ref=estimate.at[g, pl.ds(0, estimate_out.shape[2])],
            dst_ref=estimate_out.at[channel, g],
            send_sem=final_send.at[g, p],
            recv_sem=final_recv.at[g, chan - p],
            device_id={"chan": chan_peer(p)},
            device_id_type=MESH,
        )

    def update(g):
        wait_vox(slot_sums, returned, back_send, back_recv, g)
        gradient = jnp.dot(
            return_hot_ref[...],
            returned[g].astype(f32).reshape(-1, voxels).astype(bf16),
            preferred_element_type=f32,
        )
        estimate[g] = jnp.maximum(estimate[g] + steps_ref[g] * gradient, 0.0)

    turns = ITERATIONS * STREAMS

    def turn(n, carry):
        g = lax.rem(n, STREAMS)

        @pl.when(n < turns)
        def _():
            pick_tiles(g)
            apply(g)

        @pl.when(n >= 1)
        def _():
            other = lax.rem(n + STREAMS - 1, STREAMS)
            update(other)

            @pl.when(n < turns + 1 - STREAMS)
            def _():
                start_ahead(other)
                send_ahead(other)

            @pl.when(n >= turns + 1 - STREAMS)
            def _():
                for p in peers:
                    final_copy(other, p).start()
                estimate_out[channel, other] = estimate[other, 0 : estimate_out.shape[2], :]

        @pl.when(n < turns)
        def _():
            sum_slots(g)

        return carry

    lax.fori_loop(0, turns + 1, turn, 0)

    def finish(g, carry):
        for p in peers:
            landed = estimate_out.at[chan_peer(p), g]
            sent = estimate.at[g, pl.ds(0, estimate_out.shape[2])]
            pltpu.make_async_copy(landed, landed, final_recv.at[g, p]).wait()
            pltpu.make_async_copy(sent, sent, final_send.at[g, p]).wait()
        return carry

    lax.fori_loop(0, STREAMS, finish, 0)


def shards(model_blocks, start_image, measured, step_size, sent_tiles, block_rows, block_slots):
    vox, chan = lax.axis_size("vox"), lax.axis_size("chan")
    channel = lax.axis_index("chan")
    send_table = sent_tiles[0]
    capacity = send_table.shape[1]
    tile_count, wave_count, width = start_image.shape
    row_count, block_count = measured.shape[0], model_blocks.shape[0]
    waves = wave_count // chan // STREAMS
    slots = vox * capacity
    padded = -(-block_count // 16) * 16
    rows = padded * waves
    int32, bf16 = jnp.int32, jnp.bfloat16

    def flat(index, minor):
        spread = index[..., None] * minor + jnp.arange(minor, dtype=int32)
        return jnp.where(index[..., None] < 0, -1, spread).reshape(index.shape[:-1] + (-1,))

    slot_row = jnp.pad(block_slots, (0, LANES - block_count), constant_values=-1)
    slot_row = jnp.broadcast_to(slot_row[None, :], (8, LANES))
    send_code = flat(send_table.reshape(-1), waves)
    tile_range = jnp.arange(LANES)
    send_hot = (send_code[:, None] == tile_range[None, :]).astype(bf16)
    return_hot = (tile_range[:, None] == send_code[None, :]).astype(bf16)
    row_code = jnp.pad(block_rows, (0, padded - block_count), constant_values=-1)
    row_code = jnp.where(
        row_code[None, :] < 0, -1, jnp.arange(chan, dtype=int32)[:, None] * row_count + row_code[None, :]
    )
    row_code = flat(row_code, waves).reshape(-1)
    row_hot = (row_code[:, None] == jnp.arange(LANES)[None, :]).astype(bf16)
    row_sum = (jnp.arange(chan * row_count * waves)[:, None] == row_code[None, :]).astype(bf16)

    own = lax.dynamic_slice_in_dim(start_image, channel * waves * STREAMS, waves * STREAMS, axis=1)
    own = own.reshape(tile_count, STREAMS, waves, width).transpose(1, 0, 2, 3)
    own = own.reshape(STREAMS, tile_count * waves, width)
    own = jnp.pad(own, ((0, 0), (0, LANES - tile_count * waves), (0, 0)))
    steps = lax.dynamic_slice_in_dim(step_size, channel * waves * STREAMS, waves * STREAMS)
    steps = jnp.tile(steps.reshape(STREAMS, waves), (1, LANES // waves))
    steps = jnp.broadcast_to(steps[:, :, None], own.shape)
    split = measured.reshape(row_count, chan, STREAMS, waves, width).transpose(1, 2, 0, 3, 4)
    split = split.reshape(chan, STREAMS, row_count * waves, width)

    packet = (STREAMS, vox, capacity * waves, width)
    quarter = (STREAMS, chan, rows, width)
    dma = pltpu.SemaphoreType.DMA
    estimate, residual = pl.pallas_call(
        functools.partial(landweber_body, vox, chan),
        out_shape=(
            jax.ShapeDtypeStruct((chan, STREAMS, tile_count * waves, width), jnp.float32),
            jax.ShapeDtypeStruct(split.shape, jnp.float32),
        ),
        in_specs=[ANY] + [VMEM] * 8,
        out_specs=(VMEM, VMEM),
        scratch_shapes=[
            pltpu.VMEM((padded,) + model_blocks.shape[1:], bf16),
            pltpu.VMEM((chan,) + slot_row.shape, int32),
            pltpu.VMEM((chan * LANES, slots), bf16),
            pltpu.VMEM((slots, chan * LANES), bf16),
            pltpu.VMEM(own.shape, jnp.float32),
            pltpu.VMEM(packet, bf16),
            pltpu.VMEM(packet, bf16),
            pltpu.VMEM((max(slots * waves, chan * rows), width), jnp.float32),
            pltpu.VMEM(quarter, bf16),
            pltpu.VMEM(quarter, bf16),
            pltpu.VMEM((chan * rows, width), bf16),
            pltpu.VMEM((chan * rows, width), bf16),
            pltpu.VMEM((chan * rows, width), jnp.float32),
            pltpu.VMEM(quarter, bf16),
            pltpu.VMEM(quarter, bf16),
            pltpu.VMEM((chan * LANES, waves * width), bf16),
            pltpu.VMEM(packet, bf16),
            pltpu.VMEM(packet, bf16),
            dma,
            dma((chan,)),
            dma((chan,)),
            dma((STREAMS,)),
            dma((STREAMS,)),
            dma((STREAMS, chan)),
            dma((STREAMS, chan)),
            dma((STREAMS, chan)),
            dma((STREAMS, chan)),
            dma((STREAMS,)),
            dma((STREAMS,)),
            dma((STREAMS, chan)),
            dma((STREAMS, chan)),
        ],
        compiler_params=pltpu.CompilerParams(
            collective_id=0, has_side_effects=True, vmem_limit_bytes=32 << 20
        ),
        name="landweber",
    )(model_blocks, slot_row, own, split, steps, send_hot, return_hot, row_hot, row_sum)
    estimate = estimate.reshape(chan, STREAMS, tile_count, waves, width).transpose(2, 0, 1, 3, 4)
    residual = residual.reshape(chan, STREAMS, row_count, waves, width).transpose(2, 0, 1, 3, 4)
    return (
        estimate.reshape(tile_count, wave_count, width),
        residual.reshape(row_count, wave_count, width),
    )


def solution(mesh):
    in_specs = (
        P(("vox", "chan"), None, None),
        P("vox", None, None),
        P(("vox", "chan"), None, None),
        P(),
        P("vox", None, None),
        P(("vox", "chan")),
        P(("vox", "chan")),
    )
    out_specs = (P("vox", None, None), P(("vox", "chan"), None, None))
    return jax.shard_map(shards, mesh=mesh, in_specs=in_specs, out_specs=out_specs, check_vma=False)
```

```python
import functools

import jax
import jax.numpy as jnp
from jax import lax
from jax.experimental import pallas as pl
from jax.experimental.pallas import tpu as pltpu
from jax.sharding import PartitionSpec as P

ITERATIONS = 4
STREAMS = 4
PLANE = 8
LANES = 128
MESH = pl.DeviceIdType.MESH
VMEM = pl.BlockSpec(memory_space=pltpu.VMEM)
ANY = pl.BlockSpec(memory_space=pl.ANY)


def landweber_body(
    vox,
    chan,
    model_ref,
    codes_ref,
    start_ref,
    signal_ref,
    gains_ref,
    estimate_out,
    residual_out,
    held,
    begin,
    measured_ref,
    steps_ref,
    send_hot_ref,
    return_hot_ref,
    row_hot_ref,
    row_sum_ref,
    peer_slots,
    gather_hot,
    scatter_hot,
    estimate,
    outgoing,
    arrived,
    spread,
    picked,
    tiles,
    high,
    low,
    narrow,
    terms,
    group_terms,
    stacked,
    slot_sums,
    returned,
    load_sems,
    slots_send,
    slots_recv,
    ahead_send,
    ahead_recv,
    tile_send,
    tile_recv,
    term_send,
    term_recv,
    back_send,
    back_recv,
    final_send,
    final_recv,
):
    me, channel = lax.axis_index("vox"), lax.axis_index("chan")
    layer, place = me // PLANE, lax.rem(me, PLANE)
    layers = vox // PLANE
    peers = (2, 1, 3)
    padded, samples, voxels = held.shape
    block_count = model_ref.shape[0]
    rows = tiles.shape[2]
    waves = rows // padded
    pack = 8 // waves
    slot_count = scatter_hot.shape[0]
    f32, bf16 = jnp.float32, jnp.bfloat16

    def chan_peer(step):
        return lax.rem(channel + step, chan)

    barrier = pltpu.get_barrier_semaphore()

    def greet(step, carry):
        peer = lax.rem(me + step, vox)
        pl.semaphore_signal(barrier, inc=1, device_id={"vox": peer}, device_id_type=MESH)
        return carry

    lax.fori_loop(1, vox, greet, 0)
    for p in peers:
        pl.semaphore_signal(barrier, inc=1, device_id={"chan": chan_peer(p)}, device_id_type=MESH)

    tile_count, quarter_waves = begin.shape[0], begin.shape[1]
    row_count = signal_ref.shape[0]
    own_waves = pl.ds(pl.multiple_of(channel * quarter_waves, quarter_waves), quarter_waves)
    begin_load = pltpu.make_async_copy(start_ref.at[:, own_waves, :], begin, load_sems.at[0])
    begin_load.start()
    load = pltpu.make_async_copy(model_ref, held.at[pl.ds(0, block_count)], load_sems.at[1])
    load.start()

    def start_vox(source, target, send_sem, recv_sem, g):
        def send(distance):
            def one(turn, carry):
                for d in distance:
                    peer = lax.rem(layer + d, layers) * PLANE + lax.rem(place + turn, PLANE)
                    pltpu.make_async_remote_copy(
                        src_ref=source.at[g, peer],
                        dst_ref=target.at[g, me],
                        send_sem=send_sem.at[g],
                        recv_sem=recv_sem.at[g],
                        device_id={"vox": peer},
                        device_id_type=MESH,
                    ).start()
                return carry

            return one

        half = layers // 2
        lax.fori_loop(0, PLANE, send((half,)), 0)
        for d in range(half - 1, 0, -1):
            lax.fori_loop(0, PLANE, send((d, layers - d)), 0)
        lax.fori_loop(1, PLANE, send((0,)), 0)
        target[g, me] = source[g, me]

    def wait_vox(source, target, send_sem, recv_sem, g):
        others = pl.ds(0, vox - 1)
        pltpu.make_async_copy(target.at[g, others], target.at[g, others], recv_sem.at[g]).wait()
        pltpu.make_async_copy(source.at[g, others], source.at[g, others], send_sem.at[g]).wait()

    def chan_copy(source, target, send_sem, recv_sem, g, p):
        return pltpu.make_async_remote_copy(
            src_ref=source.at[g, p],
            dst_ref=target.at[g, chan - p],
            send_sem=send_sem.at[g, p],
            recv_sem=recv_sem.at[g, chan - p],
            device_id={"chan": chan_peer(p)},
            device_id_type=MESH,
        )

    def wait_chan(source, target, send_sem, recv_sem, g):
        for p in peers:
            pltpu.make_async_copy(target.at[g, p], target.at[g, p], recv_sem.at[g, p]).wait()
            pltpu.make_async_copy(source.at[g, p], source.at[g, p], send_sem.at[g, p]).wait()

    def start_ahead(g):
        slots = jnp.dot(
            send_hot_ref[...], estimate[g].astype(bf16), preferred_element_type=f32
        )
        for w in range(waves):
            spread[pl.ds(w, slot_count, stride=waves), :] = slots[
                w * slot_count : (w + 1) * slot_count
            ]
        outgoing[g] = spread[0 : slot_count * waves, :].reshape(outgoing.shape[1:]).astype(bf16)

    def send_ahead(g):
        start_vox(outgoing, arrived, ahead_send, ahead_recv, g)

    def slots_copy(p):
        return pltpu.make_async_remote_copy(
            src_ref=codes_ref,
            dst_ref=peer_slots.at[chan - p],
            send_sem=slots_send.at[p],
            recv_sem=slots_recv.at[chan - p],
            device_id={"chan": chan_peer(p)},
            device_id_type=MESH,
        )

    def ones_where(condition):
        return jnp.where(condition, 1.0, 0.0).astype(bf16)

    def iota(shape, dimension):
        return lax.broadcasted_iota(jnp.int32, shape, dimension)

    diagonal_hot = ones_where(iota((LANES, LANES), 0) == iota((LANES, LANES), 1))

    def turned(hot):
        return lax.dot_general(
            diagonal_hot, hot, (((1,), (1,)), ((), ())), preferred_element_type=f32
        ).astype(bf16)

    for w in range(waves):
        for part in range(slot_count // LANES):
            named = jnp.broadcast_to(codes_ref[2 + part : 3 + part, :], (LANES, LANES))
            target = jnp.where(named < 0, -1, named + w * tile_count)
            hot = ones_where(iota((LANES, LANES), 0) == target)
            column = w * slot_count + part * LANES
            return_hot_ref[:, column : column + LANES] = hot
            send_hot_ref[column : column + LANES, :] = turned(hot)
    estimate[...] = jnp.zeros_like(estimate)
    steps_ref[...] = jnp.zeros_like(steps_ref)
    begin_load.wait()
    for g in range(STREAMS):
        for w in range(waves):
            wave = g * waves + w
            span = slice(w * tile_count, (w + 1) * tile_count)
            estimate[g, span, :] = begin[:, wave, :]
            steps_ref[g, span, :] = jnp.full(
                (tile_count, voxels), gains_ref[channel * quarter_waves + wave], f32
            )
        start_ahead(g)
    pl.semaphore_wait(barrier, vox - 1 + chan - 1)
    for p in peers:
        slots_copy(p).start()

    def first_send(g, carry):
        send_ahead(g)
        return carry

    lax.fori_loop(0, STREAMS, first_send, 0)
    held[block_count:] = jnp.zeros((padded - block_count, samples, voxels), bf16)
    stacked[...] = jnp.zeros_like(stacked)
    peer_slots[0] = codes_ref[...]
    for p in peers:
        pltpu.make_async_copy(peer_slots.at[p], peer_slots.at[p], slots_recv.at[p]).wait()
        pltpu.make_async_copy(codes_ref, codes_ref, slots_send.at[p]).wait()
    for q in range(chan):
        for g in range(STREAMS):
            for w in range(waves):
                measured_ref[q, g, w * row_count : (w + 1) * row_count, :] = signal_ref[
                    :, q * quarter_waves + g * waves + w, :
                ]
    lanes = iota((LANES, chan * rows), 1)
    block_of = lax.div(lax.rem(lanes, rows), waves)
    row_vector = jnp.broadcast_to(codes_ref[1:2, :], (16, LANES)).astype(f32).astype(bf16)
    row_lanes = jnp.dot(
        row_vector, ones_where(iota(lanes.shape, 0) == block_of), preferred_element_type=f32
    )
    row_lanes = jnp.broadcast_to(row_lanes[0:1, :], lanes.shape).astype(jnp.int32)
    target = (lax.div(lanes, rows) * waves + lax.rem(lanes, waves)) * row_count + row_lanes
    row_sum_ref[...] = ones_where(iota(lanes.shape, 0) == jnp.where(row_lanes < 0, -1, target))
    for part in range(chan * rows // LANES):
        span = slice(part * LANES, (part + 1) * LANES)
        row_hot_ref[span, :] = turned(row_sum_ref[:, span])
    slot_range = iota((slot_count, LANES), 0)
    for p in range(chan):
        span = slice(p * LANES, (p + 1) * LANES)
        named = jnp.broadcast_to(peer_slots[p][0:1, :], slot_range.shape)
        hot = ones_where(slot_range == named)
        scatter_hot[:, span] = hot
        gather_hot[span, :] = turned(hot)
    load.wait()

    group_of = lax.broadcasted_iota(jnp.int32, (8, voxels), 0) // waves

    def diagonal(product, p):
        part = slice(8 * p, 8 * p + 8)
        piece = product[part, 0:voxels]
        for i in range(1, pack):
            piece = jnp.where(group_of == i, product[part, i * voxels : (i + 1) * voxels], piece)
        return piece

    def pick_tiles(g):
        wait_vox(outgoing, arrived, ahead_send, ahead_recv, g)
        spread[0 : slot_count * waves, :] = arrived[g].astype(f32).reshape(-1, voxels)
        source = jnp.concatenate(
            [spread[pl.ds(w, slot_count, stride=waves), :] for w in range(waves)], axis=1
        ).astype(bf16)
        product = jnp.dot(gather_hot[...], source, preferred_element_type=f32)
        for p in peers + (0,):
            for w in range(waves):
                spread[pl.ds(p * rows + w, padded, stride=waves), :] = product[
                    p * LANES : p * LANES + padded, w * voxels : (w + 1) * voxels
                ]
            part = spread[p * rows : (p + 1) * rows, :].astype(bf16)
            if p == 0:
                tiles[g, 0] = part
            else:
                picked[g, p] = part
                chan_copy(picked, tiles, tile_send, tile_recv, g, p).start()

    def apply(g):
        wait_chan(picked, tiles, tile_send, tile_recv, g)
        for q in range(rows // 16):
            wide = [tiles[g, p, 16 * q : 16 * q + 16, :].astype(f32) for p in range(chan)]
            halves = []
            for h in range(2):
                left = jnp.concatenate([w[8 * h : 8 * h + 8] for w in wide], axis=0).astype(bf16)
                k = (2 * q + h) * pack
                right = held[k : k + pack].reshape(pack * samples, voxels)
                product = lax.dot_general(
                    left, right, (((1,), (1,)), ((), ())), preferred_element_type=f32
                )
                halves.append([diagonal(product, p) for p in range(chan)])
            for p in range(chan):
                piece = jnp.concatenate([halves[0][p], halves[1][p]], axis=0)
                top = piece.astype(bf16)
                where = slice(p * rows + 16 * q, p * rows + 16 * q + 16)
                high[where, :] = top
                low[where, :] = (piece - top.astype(f32)).astype(bf16)
        predicted = jnp.dot(row_sum_ref[...], high[...], preferred_element_type=f32)
        predicted += jnp.dot(row_sum_ref[...], low[...], preferred_element_type=f32)
        part = waves * row_count
        residuals = []
        for p in range(chan):
            residual = measured_ref[chan_peer(p), g] - predicted[p * part : (p + 1) * part]
            residual_out[chan_peer(p), g] = residual
            residuals.append(residual.astype(bf16))
        residuals.append(jnp.zeros((LANES - chan * part, samples), bf16))
        narrow[...] = jnp.dot(
            row_hot_ref[...], jnp.concatenate(residuals, axis=0), preferred_element_type=f32
        )
        for q in range(rows // 16):
            halves = []
            for h in range(2):
                k = (2 * q + h) * pack
                left = jnp.concatenate(
                    [
                        narrow[p * rows + 16 * q + 8 * h : p * rows + 16 * q + 8 * h + 8, :]
                        for p in range(chan)
                    ],
                    axis=0,
                ).astype(bf16)
                right = jnp.concatenate([held[k + i] for i in range(pack)], axis=1)
                product = jnp.dot(left, right, preferred_element_type=f32)
                halves.append([diagonal(product, p) for p in range(chan)])
            for p in range(chan):
                piece = jnp.concatenate([halves[0][p], halves[1][p]], axis=0).astype(bf16)
                if p == 0:
                    group_terms[g, 0, 16 * q : 16 * q + 16, :] = piece
                else:
                    terms[g, p, 16 * q : 16 * q + 16, :] = piece
        for p in peers:
            chan_copy(terms, group_terms, term_send, term_recv, g, p).start()

    def sum_slots(g):
        wait_chan(terms, group_terms, term_send, term_recv, g)
        for p in range(chan):
            spread[p * rows : (p + 1) * rows, :] = group_terms[g, p].astype(f32)
            for w in range(waves):
                stacked[p * LANES : p * LANES + padded, w * voxels : (w + 1) * voxels] = spread[
                    pl.ds(p * rows + w, padded, stride=waves), :
                ].astype(bf16)
        product = jnp.dot(scatter_hot[...], stacked[...], preferred_element_type=f32)
        for w in range(waves):
            spread[pl.ds(w, slot_count, stride=waves), :] = product[:, w * voxels : (w + 1) * voxels]
        slot_sums[g] = (
            spread[0 : slot_count * waves, :].reshape(slot_sums.shape[1:]).astype(bf16)
        )
        start_vox(slot_sums, returned, back_send, back_recv, g)

    def final_copy(g, p):
        return pltpu.make_async_remote_copy(
            src_ref=estimate.at[g, pl.ds(0, estimate_out.shape[2])],
            dst_ref=estimate_out.at[channel, g],
            send_sem=final_send.at[g, p],
            recv_sem=final_recv.at[g, chan - p],
            device_id={"chan": chan_peer(p)},
            device_id_type=MESH,
        )

    def update(g):
        wait_vox(slot_sums, returned, back_send, back_recv, g)
        spread[0 : slot_count * waves, :] = returned[g].astype(f32).reshape(-1, voxels)
        source = jnp.concatenate(
            [spread[pl.ds(w, slot_count, stride=waves), :] for w in range(waves)], axis=0
        ).astype(bf16)
        gradient = jnp.dot(
            return_hot_ref[...],
            source,
            preferred_element_type=f32,
        )
        estimate[g] = jnp.maximum(estimate[g] + steps_ref[g] * gradient, 0.0)

    turns = ITERATIONS * STREAMS

    def turn(n, carry):
        @pl.when(n < turns)
        def _():
            pick_tiles(lax.rem(n, STREAMS))

        @pl.when((n >= 1) & (n < turns + 1))
        def _():
            sum_slots(lax.rem(n + STREAMS - 1, STREAMS))

        @pl.when(n < turns)
        def _():
            apply(lax.rem(n, STREAMS))

        @pl.when(n >= 2)
        def _():
            g = lax.rem(n + STREAMS - 2, STREAMS)
            update(g)

            @pl.when(n < turns + 2 - STREAMS)
            def _():
                start_ahead(g)
                send_ahead(g)

            @pl.when(n >= turns + 2 - STREAMS)
            def _():
                for p in peers:
                    final_copy(g, p).start()
                estimate_out[channel, g] = estimate[g, 0 : estimate_out.shape[2], :]

        return carry

    lax.fori_loop(0, turns + 2, turn, 0)

    def finish(g, carry):
        for p in peers:
            landed = estimate_out.at[chan_peer(p), g]
            sent = estimate.at[g, pl.ds(0, estimate_out.shape[2])]
            pltpu.make_async_copy(landed, landed, final_recv.at[g, p]).wait()
            pltpu.make_async_copy(sent, sent, final_send.at[g, p]).wait()
        return carry

    lax.fori_loop(0, STREAMS, finish, 0)


def shards(model_blocks, start_image, measured, step_size, sent_tiles, block_rows, block_slots):
    vox, chan = lax.axis_size("vox"), lax.axis_size("chan")
    send_table = sent_tiles[0]
    capacity = send_table.shape[1]
    tile_count, wave_count, width = start_image.shape
    row_count, block_count = measured.shape[0], model_blocks.shape[0]
    waves = wave_count // chan // STREAMS
    slots = vox * capacity
    padded = -(-block_count // 16) * 16
    rows = padded * waves
    int32, bf16 = jnp.int32, jnp.bfloat16

    codes = jnp.pad(
        jnp.stack([block_slots, block_rows]), ((0, 0), (0, LANES - block_count)), constant_values=-1
    )
    table = send_table.reshape(slots // LANES, LANES)
    codes = jnp.concatenate([codes, table, jnp.zeros((6 - slots // LANES, LANES), int32)])

    signals = (chan, STREAMS, waves * row_count, width)
    estimates = (STREAMS, LANES, width)
    packet = (STREAMS, vox, capacity * waves, width)
    quarter = (STREAMS, chan, rows, width)
    dma = pltpu.SemaphoreType.DMA
    estimate, residual = pl.pallas_call(
        functools.partial(landweber_body, vox, chan),
        out_shape=(
            jax.ShapeDtypeStruct((chan, STREAMS, tile_count * waves, width), jnp.float32),
            jax.ShapeDtypeStruct(signals, jnp.float32),
        ),
        in_specs=[ANY, VMEM, ANY, VMEM, pl.BlockSpec(memory_space=pltpu.SMEM)],
        out_specs=(VMEM, VMEM),
        scratch_shapes=[
            pltpu.VMEM((padded,) + model_blocks.shape[1:], bf16),
            pltpu.VMEM((tile_count, wave_count // chan, width), jnp.float32),
            pltpu.VMEM(signals, jnp.float32),
            pltpu.VMEM(estimates, jnp.float32),
            pltpu.VMEM((slots * waves, LANES), bf16),
            pltpu.VMEM((LANES, slots * waves), bf16),
            pltpu.VMEM((chan * rows, LANES), bf16),
            pltpu.VMEM((LANES, chan * rows), bf16),
            pltpu.VMEM((chan,) + codes.shape, int32),
            pltpu.VMEM((chan * LANES, slots), bf16),
            pltpu.VMEM((slots, chan * LANES), bf16),
            pltpu.VMEM(estimates, jnp.float32),
            pltpu.VMEM(packet, bf16),
            pltpu.VMEM(packet, bf16),
            pltpu.VMEM((max(slots * waves, chan * rows), width), jnp.float32),
            pltpu.VMEM(quarter, bf16),
            pltpu.VMEM(quarter, bf16),
            pltpu.VMEM((chan * rows, width), bf16),
            pltpu.VMEM((chan * rows, width), bf16),
            pltpu.VMEM((chan * rows, width), jnp.float32),
            pltpu.VMEM(quarter, bf16),
            pltpu.VMEM(quarter, bf16),
            pltpu.VMEM((chan * LANES, waves * width), bf16),
            pltpu.VMEM(packet, bf16),
            pltpu.VMEM(packet, bf16),
            dma((2,)),
            dma((chan,)),
            dma((chan,)),
            dma((STREAMS,)),
            dma((STREAMS,)),
            dma((STREAMS, chan)),
            dma((STREAMS, chan)),
            dma((STREAMS, chan)),
            dma((STREAMS, chan)),
            dma((STREAMS,)),
            dma((STREAMS,)),
            dma((STREAMS, chan)),
            dma((STREAMS, chan)),
        ],
        compiler_params=pltpu.CompilerParams(
            collective_id=0, has_side_effects=True, vmem_limit_bytes=32 << 20
        ),
        name="landweber",
    )(model_blocks, codes, start_image, measured, step_size)
    estimate = estimate.reshape(chan, STREAMS, waves, tile_count, width).transpose(3, 0, 1, 2, 4)
    residual = residual.reshape(chan, STREAMS, waves, row_count, width).transpose(3, 0, 1, 2, 4)
    return (
        estimate.reshape(tile_count, wave_count, width),
        residual.reshape(row_count, wave_count, width),
    )


def solution(mesh):
    in_specs = (
        P(("vox", "chan"), None, None),
        P("vox", None, None),
        P(("vox", "chan"), None, None),
        P(),
        P("vox", None, None),
        P(("vox", "chan")),
        P(("vox", "chan")),
    )
    out_specs = (P("vox", None, None), P(("vox", "chan"), None, None))
    return jax.shard_map(shards, mesh=mesh, in_specs=in_specs, out_specs=out_specs, check_vma=False)
```
